32 devices in a mesh: lon: 4 (over x, core), frame: 8 (over z, y).
Axes of the slice: x: 2, y: 2, z: 4, core: 2. Of those that a mesh axis runs over, the one named last changes fastest.
Arguments:
- layer_input: bfloat16 [8, 16, 512, 128], P('frame', None, 'lon'), may hold values from -6 to 6
- hidden_saved: bfloat16 [8, 16, 512, 128], P('frame', None, 'lon'), as said below
- conv_weight: bfloat16 [3, 3, 128, 128], replicated, may hold values from -0.1875 to 0.1875
- queries: bfloat16 [2048, 128], P('lon'), may hold values from -6 to 6
- corr_cotangent: bfloat16 [8, 49, 2048], P('frame', None, 'lon'), may hold values from -0.59765625 to 0.59765625
- window_rows: int32 [8, 2048], P('frame', 'lon'), may hold values from 0 to 9
- window_cols: int32 [8, 2048], P('frame', 'lon'), may hold values from -3 to 124
- owner_strip: int32 [8, 2048, 1], P('frame', 'lon'), may hold values from 0 to 3; in each aligned block of 512 rows (0 to 511, 512 to 1023, ..., all dimensions but the last counted through in order) at most 128 rows name the same one
Outputs:
- query_grad: float32 [2048, 128], P(('lon', 'frame'))
- first_weight_grad: float32 [3, 3, 128, 128], replicated
- second_weight_grad: float32 [3, 3, 128, 128], replicated
The draws below stay inside these ranges and needn't reach their ends.
Inputs may be any that keep to these rules, and one draw needn't show every extreme that they name: `hidden_saved`: rectifier outputs: zero or positive, a third or more of them exactly zero. `owner_strip`: in each frame, at most 128 of the 512 tracks homed on one strip name the same owning strip.
All inputs are finite; a program needn't handle non-finite values.
Results may differ from the reference program's by a relative error of at most 0.0045.
Values may be sent and summed in bfloat16 or wider, within the bound.
A program may use at most 64 MiB of HBM per device.

```python
import math
import jax
import jax.numpy as jnp
import numpy as np
from jax import lax

C = 128
WIN = 7
ROWS = 16
COLS = 128
TRK_DEV = 512
FRAMES = 8
WIDTH = 512
TRACKS = 2048
CAP = 128
N_LON = 4


def draw_hidden_saved(key, part):
    values = jax.random.normal(key, (FRAMES, ROWS, WIDTH, C), jnp.float32)
    return jnp.maximum(values, 0.0).astype(jnp.bfloat16)


def place_ends(entries, rng, smallest, high):
    longest = entries.shape.index(max(entries.shape))
    spots = []
    for shift in (0, 1):
        where = [jax.random.randint(jax.random.fold_in(rng, axis), (), 0, length) for axis, length in enumerate(entries.shape)]
        where[longest] = (where[longest] + shift) % entries.shape[longest]
        spots.append(tuple(where))
    return entries.at[spots[0]].set(smallest).at[spots[1]].set(high)


def steps_of(rng, shape, cuts, low, largest):
    def one(dim, shards_of):
        steps = jax.random.uniform(jax.random.fold_in(jax.random.fold_in(rng, 6), dim), (shards_of,), jnp.float32, low / len(cuts), largest / len(cuts))
        return jnp.repeat(jnp.exp(steps), shape[dim] // shards_of).reshape((-1,) + (1,) * (len(shape) - dim - 1))

    factor_of = one(*cuts[0])
    for cut in cuts[1:]:
        factor_of = factor_of * one(*cut)
    return factor_of


def shared_out(key, own, number, rows, number_of, top, bound, lean):
    ranking = jax.random.permutation(key, number_of)
    crowded, ordinary = load_shares(number_of, rows * top, bound, lean, True), load_shares(number_of, rows * top, bound, lean, False)
    places = jnp.arange(number_of)

    def named(tallies, turn):
        used = int((tallies > 0).sum())
        fixed = max(1, used // 4)
        passed = fixed + (places - fixed + turn * (used - fixed)) % max(1, number_of - fixed)
        return jnp.zeros((number_of,), jnp.int32).at[ranking[jnp.where(places < fixed, places, passed)]].set(jnp.asarray(tallies, jnp.int32))

    tallies = jnp.where(number % 4 == 0, named(crowded, number // 4), named(ordinary, number - number // 4 - 1))
    mixed = jax.random.permutation(jax.random.fold_in(own, 3), number_of)
    giver, taker = mixed[0:number_of // 2 * 2:2], mixed[1:number_of // 2 * 2:2]
    margin = jnp.minimum(tallies[giver] - 1, bound - tallies[taker]) // 2
    margin = jnp.where((giver == ranking[0]) | (taker == ranking[0]) | (tallies[taker] == 0), 0, jnp.maximum(margin, 0))
    passed = jax.random.randint(jax.random.fold_in(own, 4), (number_of // 2,), 0, 1 << 20) % (margin + 1)
    tallies = tallies.at[giver].add(-passed).at[taker].add(passed)
    labels = jnp.searchsorted(jnp.cumsum(tallies), jnp.arange(rows * top), side="right").astype(jnp.int32)
    table = labels.reshape(top, rows).T
    table = table[jax.random.permutation(jax.random.fold_in(own, 1), rows)]
    turn = jax.random.randint(jax.random.fold_in(own, 2), (rows, 1), 0, top)
    return jnp.take_along_axis(table, (jnp.arange(top)[None, :] + turn) % top, axis=1)


def load_shares(amount, total, limit, lean, full):
    portions = [(1 << 20) // math.isqrt(standing ** lean) + 1 for standing in range(1, amount + 1)]
    largest = limit if full else min(limit, max(-(-total // amount), total * portions[0] // sum(portions)))
    least = 1 if total - largest >= amount - 1 else 0
    counts, surplus = [largest] + [least] * (amount - 1), total - largest - least * (amount - 1)
    while surplus > 0:
        candidates = [i for i in range(1, amount) if counts[i] < largest] or [i for i in range(1, amount) if counts[i] < limit]
        whole, budget = sum([portions[i] for i in candidates]), surplus
        for i in candidates:
            extra = min(limit - counts[i], max(1, budget * portions[i] // whole), surplus)
            counts[i] = counts[i] + extra
            surplus = surplus - extra
    return np.array(counts)


def bell_draw(stream_key, shape, deviation, limit, cuts=(), dtype=jnp.bfloat16):
    gain = steps_of(stream_key, shape, cuts, -0.22, 0.18) if cuts else 1.0
    drawn = jax.random.normal(stream_key, shape, jnp.float32) * deviation * gain
    return jnp.minimum(jnp.maximum(drawn, -limit), limit).astype(dtype)


def setup_inputs(seed: int = 0) -> dict:
    seeds = jax.random.split(jax.random.key(seed), 9)
    layer_input = bell_draw(seeds[0], (FRAMES, ROWS, WIDTH, C), 1.0, 6.0, ((0, 8), (2, 4)))
    hidden_saved = draw_hidden_saved(jax.random.fold_in(seeds[8], 71), 0)
    conv_weight = bell_draw(seeds[2], (3, 3, C, C), (9 * C) ** -0.5, 0.1875)
    queries = bell_draw(seeds[3], (TRACKS, C), 1.0, 6.0, ((0, 4),))
    corr_cotangent = bell_draw(seeds[4], (FRAMES, WIN * WIN, TRACKS), 0.1, 0.59765625, ((0, 8), (2, 4)))
    window_rows = place_ends(jax.random.randint(seeds[5], (FRAMES, TRACKS), 0, ROWS - WIN + 1), jax.random.fold_in(seeds[5], 1), 0, ROWS - WIN).astype(jnp.int32)
    window_cols = place_ends(jax.random.randint(seeds[6], (FRAMES, TRACKS), -3, COLS - 3), jax.random.fold_in(seeds[6], 1), -3, (COLS - 3) - 1).astype(jnp.int32)
    owner_strip_keys = jax.random.split(jax.random.fold_in(seeds[7], 1), FRAMES * TRACKS // TRK_DEV)
    owner_strip_turns = jax.random.permutation(jax.random.fold_in(seeds[7], 3), FRAMES * TRACKS // TRK_DEV)
    owner_strip = jax.vmap(lambda own, number: shared_out(jax.random.fold_in(seeds[7], 2), own, number, TRK_DEV, N_LON, 1, CAP, 2))(owner_strip_keys, owner_strip_turns).reshape((FRAMES, TRACKS, 1))
    return {"layer_input": layer_input, "hidden_saved": hidden_saved, "conv_weight": conv_weight, "queries": queries, "corr_cotangent": corr_cotangent, "window_rows": window_rows, "window_cols": window_cols, "owner_strip": owner_strip}


exact_mode = lax.Precision.HIGHEST

def pad_cells(field):
    padded_rows = jnp.pad(field, ((1, 1), (0, 0), (0, 0)))
    return jnp.concatenate([padded_rows[:, -1:], padded_rows, padded_rows[:, :1]], axis=1)

def forward_conv(padded, weight):
    result = jnp.zeros((ROWS, WIDTH, C), jnp.float32)
    for row_tap in range(3):
        for col_tap in range(3):
            window = padded[row_tap:row_tap + ROWS, col_tap:col_tap + WIDTH]
            result = result + jnp.einsum('rci,io->rco', window, weight[row_tap, col_tap], precision=exact_mode)
    return result

def backward_conv(padded, weight):
    result = jnp.zeros((ROWS, WIDTH, C), jnp.float32)
    for row_tap in range(3):
        for col_tap in range(3):
            window = padded[2 - row_tap:2 - row_tap + ROWS, 2 - col_tap:2 - col_tap + WIDTH]
            result = result + jnp.einsum('rco,io->rci', window, weight[row_tap, col_tap], precision=exact_mode)
    return result

def weight_terms(padded, grad):
    tap_rows = []
    for row_tap in range(3):
        tap_cols = []
        for col_tap in range(3):
            window = padded[row_tap:row_tap + ROWS, col_tap:col_tap + WIDTH]
            tap_cols.append(jnp.einsum('rci,rco->io', window, grad, precision=exact_mode))
        tap_rows.append(jnp.stack(tap_cols))
    return jnp.stack(tap_rows)

def reference(layer_input, hidden_saved, conv_weight, queries, corr_cotangent, window_rows, window_cols, owner_strip):
    weight_full = conv_weight.astype(jnp.float32)
    query_full = queries.astype(jnp.float32)

    def frame_step(carry, frame_items):
        query_acc, first_acc, second_acc = carry
        input_frame, hidden_frame, cotangent, start_rows, start_cols, owners = frame_items
        hidden_padded = pad_cells(hidden_frame.astype(jnp.float32))
        feature = forward_conv(hidden_padded, weight_full).astype(jnp.bfloat16)
        feature = lax.optimization_barrier(feature).astype(jnp.float32)
        base_cols = owners * COLS + start_cols
        feature_grad = jnp.zeros((ROWS, WIDTH, C), jnp.float32)
        query_frame = jnp.zeros((TRACKS, C), jnp.float32)
        for row_off in range(WIN):
            for col_off in range(WIN):
                target_rows = (start_rows + row_off).astype(jnp.int32)
                target_cols = jnp.remainder(base_cols + col_off, WIDTH).astype(jnp.int32)
                weights_here = cotangent[row_off * WIN + col_off].astype(jnp.float32)
                query_frame = query_frame + weights_here[:, None] * feature[target_rows, target_cols]
                feature_grad = feature_grad.at[target_rows, target_cols].add(weights_here[:, None] * query_full)
        grad_rounded = lax.optimization_barrier(feature_grad.astype(jnp.bfloat16)).astype(jnp.float32)
        hidden_grad = backward_conv(pad_cells(grad_rounded), weight_full)
        pre_grad = jnp.where(hidden_frame > 0, hidden_grad, jnp.zeros_like(hidden_grad)).astype(jnp.bfloat16)
        pre_grad = lax.optimization_barrier(pre_grad).astype(jnp.float32)
        second_acc = second_acc + weight_terms(hidden_padded, grad_rounded)
        first_acc = first_acc + weight_terms(pad_cells(input_frame.astype(jnp.float32)), pre_grad)
        return ((query_acc + query_frame, first_acc, second_acc), None)
    start = (jnp.zeros((TRACKS, C), jnp.float32), jnp.zeros((3, 3, C, C), jnp.float32), jnp.zeros((3, 3, C, C), jnp.float32))
    frame_items = (layer_input, hidden_saved, corr_cotangent, window_rows, window_cols, owner_strip[:, :, 0])
    (query_grad, first_sum, second_sum), unused = lax.scan(frame_step, start, frame_items)
    norm_factor = 1.0 / math.sqrt(FRAMES * ROWS * WIDTH)
    return (query_grad, first_sum * norm_factor, second_sum * norm_factor)
```

```python
import functools
import math

import jax
import jax.numpy as jnp
from jax import lax
from jax.experimental import pallas as pl
from jax.experimental.pallas import tpu as pltpu
from jax.sharding import PartitionSpec as P

WIN = 7
WIDE = 144
EXT = 160
BF = jnp.bfloat16
F32 = jnp.float32
MESH = pl.DeviceIdType.MESH


def dot(a, b):
    return jnp.dot(a, b, preferred_element_type=F32)


def kernel(
    dims,
    x_ref, h_ref, w_ref, q_ref, cot_ref, rows_ref, cols_ref, own_ref,
    query_out, first_out, second_out,
    hext, xext, gext, xh, xx, xg, feat, wb, fgrad, gt, spread,
    cm, pt, qall, cmall,
    pay_send, pay_recv, halo_send, halo_recv, edge_send, edge_recv,
    ret_send, ret_recv, retall, qg_send, qg_own, qg_recv,
    grads, w1_send, w1_recv, acc, w2_own, w2_send, w2_recv, ag1, ag2, wide_out,
    pay_s, pay_r, halo_s, halo_r, edge_s, edge_r, ret_s, ret_r, qg_s, qg_r,
    w1_s, w1_r, w2_s, w2_r, a1_s, a1_r, a2_s, a2_r,
):
    lon_n, frame_n, rows_n, cols_n, chans, tracks, cap, chunk, scale = dims
    lon, frame = lax.axis_index("lon"), lax.axis_index("frame")
    slots = lon_n * cap
    half = rows_n // 2

    def lon_id(steps):
        return lax.rem(lon + steps + lon_n, lon_n)

    def frame_id(steps):
        return lax.rem(frame + steps + frame_n, frame_n)

    def remote(src, dst, send, recv, where):
        return pltpu.make_async_remote_copy(
            src_ref=src, dst_ref=dst, send_sem=send, recv_sem=recv,
            device_id=where, device_id_type=MESH,
        )

    barrier = pltpu.get_barrier_semaphore()
    for step in range(1, lon_n):
        pl.semaphore_signal(barrier, inc=1, device_id={"lon": lon_id(step)}, device_id_type=MESH)
    for step in range(1, frame_n):
        pl.semaphore_signal(barrier, inc=1, device_id={"frame": frame_id(step)}, device_id_type=MESH)

    halo_send[...] = jnp.zeros_like(halo_send)
    halo_send[0, :, 0:4] = h_ref[:, cols_n - 8 :].astype(F32)[:, 4:8].astype(BF)
    halo_send[0, :, 4:5] = x_ref[:, cols_n - 8 :].astype(F32)[:, 7:8].astype(BF)
    halo_send[1, :, 0:4] = h_ref[:, 0:8].astype(F32)[:, 0:4].astype(BF)
    halo_send[1, :, 4:5] = x_ref[:, 0:8].astype(F32)[:, 0:1].astype(BF)

    owners = own_ref[...]
    marks = (owners == lax.broadcasted_iota(jnp.int32, (16, tracks), 0)).astype(F32)
    earlier = (
        lax.broadcasted_iota(jnp.int32, (tracks, tracks), 0)
        < lax.broadcasted_iota(jnp.int32, (tracks, tracks), 1)
    ).astype(F32).astype(BF)
    before = dot(marks.astype(BF), earlier)
    rank = jnp.sum(before * marks, axis=0, keepdims=True).astype(jnp.int32)
    slot = owners * cap + rank
    cm[...] = jnp.zeros_like(cm)
    for i in range(WIN):
        cm[8 * i : 8 * i + WIN, :] = cot_ref[WIN * i : WIN * i + WIN, :].astype(F32)
    cm[56:57, :] = rows_ref[...].astype(F32)
    cm[57:58, :] = (cols_ref[...] + 3).astype(F32)
    cm_half = cm[...].astype(BF)

    pl.semaphore_wait(barrier, lon_n - 1 + frame_n - 1)
    halos = [
        remote(halo_send.at[0], halo_recv.at[0], halo_s.at[0], halo_r.at[0], {"lon": lon_id(1)}),
        remote(halo_send.at[1], halo_recv.at[1], halo_s.at[1], halo_r.at[1], {"lon": lon_id(-1)}),
    ]
    for copy in halos:
        copy.start()
    pays = []
    for step in list(range(1, lon_n)) + [0]:
        local = slot - lon_id(step) * cap
        hot = (local == lax.broadcasted_iota(jnp.int32, (cap, tracks), 0)).astype(F32).astype(BF)
        pt[step * cap : (step + 1) * cap, :] = hot
        q_part = dot(hot, q_ref[...]).astype(BF)
        c_part = lax.dot_general(
            cm_half, hot, (((1,), (1,)), ((), ())), preferred_element_type=F32
        )
        if step:
            pay_send[step - 1, 0:cap, :] = q_part
            pay_send[step - 1, cap : cap + 64, :] = c_part.astype(BF)
            copy = remote(
                pay_send.at[step - 1], pay_recv.at[step - 1], pay_s.at[step - 1],
                pay_r.at[step - 1], {"lon": lon_id(step)},
            )
            copy.start()
            pays.append(copy)
        else:
            qall[0:cap, :] = q_part
            cmall[:, 0:cap] = c_part

    for a in range(3):
        for b in range(3):
            tap = w_ref[2 - a, (2 - b) * chans : (3 - b) * chans, :].astype(F32)
            wb[a, b * chans : (b + 1) * chans, :] = tap.T.astype(BF)

    def fill(ext, src):
        ext[...] = jnp.zeros_like(ext)

        @pl.loop(0, rows_n)
        def _(r):
            ext[r + 1, 16 : 16 + cols_n, :] = src[r].astype(F32)

    def side_by_side(ext, out):
        @pl.loop(0, rows_n + 2)
        def _(r):
            for b in range(3):
                out[r, :, b * chans : (b + 1) * chans] = ext[r, 7 + b : 7 + b + WIDE, :].astype(BF)

    fill(hext, h_ref)
    fill(xext, x_ref)
    for copy in halos:
        copy.wait()
    prior = halo_recv[0].astype(F32)
    later = halo_recv[1].astype(F32)
    hext[1 : rows_n + 1, 12:16, :] = prior[:, 0:4]
    hext[1 : rows_n + 1, 16 + cols_n : 20 + cols_n, :] = later[:, 0:4]
    xext[1 : rows_n + 1, 15:16, :] = prior[:, 4:5]
    xext[1 : rows_n + 1, 16 + cols_n : 17 + cols_n, :] = later[:, 4:5]
    side_by_side(hext, xh)

    def conv(source, weight, r0):
        total = None
        for a in range(3):
            block = source[r0 + a : r0 + a + half].reshape(half * WIDE, 3 * chans)
            term = dot(block, weight[a])
            total = term if total is None else total + term
        return total

    for g in range(2):
        feat[g * half * WIDE : (g + 1) * half * WIDE, :] = conv(xh, w_ref, g * half).astype(BF)
    side_by_side(xext, xx)

    def spread_block(step):
        lanes = slice(step * cap, (step + 1) * cap)
        rows_t = cmall[56:57, lanes].astype(jnp.int32)
        cols_t = cmall[57:58, lanes].astype(jnp.int32) + 5
        placed = []
        for r in range(rows_n):
            value = jnp.zeros((8, cap), F32)
            for i in range(WIN):
                if 0 <= r - i <= rows_n - WIN:
                    value = jnp.where(rows_t == r - i, cmall[8 * i : 8 * i + 8, lanes], value)
            placed.append(value)

        @pl.loop(0, WIDE // 16)
        def _(tile):
            offset = lax.broadcasted_iota(jnp.int32, (16, cap), 0) + tile * 16 - cols_t
            hits = [offset == j for j in range(WIN)]
            for r in range(rows_n):
                value = jnp.zeros((16, cap), F32)
                for j in range(WIN):
                    value = jnp.where(hits[j], placed[r][j : j + 1, :], value)
                start = pl.multiple_of(r * WIDE + tile * 16, 16)
                spread[pl.ds(start, 16), lanes] = value.astype(BF)

    spread_block(0)
    for step in range(1, lon_n):
        pays[step - 1].wait()
        qall[step * cap : (step + 1) * cap, :] = pay_recv[step - 1, 0:cap, :]
        cmall[:, step * cap : (step + 1) * cap] = pay_recv[step - 1, cap : cap + 64, :].astype(F32)
        spread_block(step)

    for g in range(2):
        cells = slice(g * half * WIDE, (g + 1) * half * WIDE)
        fgrad[g * half : (g + 1) * half] = dot(spread[cells, :], qall[...]).reshape(
            half, WIDE, chans
        )
    edge_send[0, :, 0:4] = fgrad[:, 7 + cols_n : 11 + cols_n, :]
    edge_send[1, :, 0:4] = fgrad[:, 5:9, :]
    edge_send[:, :, 4:8] = jnp.zeros((2, rows_n, 4, chans), F32)
    edges = [
        remote(edge_send.at[0], edge_recv.at[0], edge_s.at[0], edge_r.at[0], {"lon": lon_id(1)}),
        remote(edge_send.at[1], edge_recv.at[1], edge_s.at[1], edge_r.at[1], {"lon": lon_id(-1)}),
    ]
    for copy in edges:
        copy.start()

    slot_grads = lax.dot_general(
        feat[...], spread[...], (((0,), (0,)), ((), ())), preferred_element_type=F32
    )
    retall[:, 0:cap] = slot_grads[:, 0:cap].astype(BF)
    returns = []
    for step in range(1, lon_n):
        ret_send[step - 1] = slot_grads[:, step * cap : (step + 1) * cap].astype(BF)
        copy = remote(
            ret_send.at[step - 1], ret_recv.at[step - 1], ret_s.at[step - 1],
            ret_r.at[step - 1], {"lon": lon_id(-step)},
        )
        copy.start()
        returns.append(copy)

    gext[...] = jnp.zeros_like(gext)
    for copy in edges:
        copy.wait()
    gext[1 : rows_n + 1, 16 : 16 + cols_n, :] = fgrad[:, 8 : 8 + cols_n, :]
    gext[1 : rows_n + 1, 15:19, :] = fgrad[:, 7:11, :] + edge_recv[0, :, 0:4]
    gext[1 : rows_n + 1, 13 + cols_n : 17 + cols_n, :] = (
        fgrad[:, 5 + cols_n : 9 + cols_n, :] + edge_recv[1, :, 0:4]
    )
    side_by_side(gext, xg)

    column = lax.broadcasted_iota(jnp.int32, (half, WIDE, chans), 1)
    inside = (column >= 8) & (column < 8 + cols_n)

    def weight_terms(which, source):
        for a in range(3):
            block = source[a : a + rows_n].reshape(rows_n * WIDE, 3 * chans)
            term = dot(gt[...], block) * scale
            for b in range(3):
                tap = term[:, b * chans : (b + 1) * chans].T
                grads[which, 3 * a + b] = tap
                for d in range(lon_n):
                    part = tap[d * (chans // lon_n) : (d + 1) * (chans // lon_n), :]
                    w1_send[which, d, 3 * a + b] = part.astype(BF)
        copies = []
        for step in range(1, lon_n):
            copy = remote(
                w1_send.at[which, lon_id(step)], w1_recv.at[which, step - 1],
                w1_s.at[which, step - 1], w1_r.at[which, step - 1], {"lon": lon_id(step)},
            )
            copy.start()
            copies.append(copy)
        return copies

    def over_frames(which, copies):
        part = chans // lon_n
        total = grads[which, :, pl.ds(pl.multiple_of(lon * part, part), part), :]
        for step in range(1, lon_n):
            copies[step - 1].wait()
            total = total + w1_recv[which, step - 1].astype(F32)
        if chunk * frame_n > 9 * part:
            acc[...] = jnp.zeros_like(acc)
        acc[0 : 9 * part, :] = total.reshape(9 * part, chans)
        for f in range(frame_n):
            piece = acc[f * chunk : (f + 1) * chunk, :]
            w2_own[which, f] = piece
            w2_send[which, f] = piece.astype(BF)
        out = []
        for step in range(1, frame_n):
            copy = remote(
                w2_send.at[which, frame_id(step)], w2_recv.at[which, step - 1],
                w2_s.at[which, step - 1], w2_r.at[which, step - 1], {"frame": frame_id(step)},
            )
            copy.start()
            out.append(copy)
        return out

    def gather_frames(which, copies):
        total = w2_own[which, frame]
        for step in range(1, frame_n):
            copies[step - 1].wait()
            total = total + w2_recv[which, step - 1].astype(F32)
        ag1[which, 0] = total.astype(BF)
        out = []
        for step in range(1, frame_n):
            copy = remote(
                ag1.at[which, 0], ag1.at[which, step],
                a1_s.at[which, step - 1], a1_r.at[which, step - 1], {"frame": frame_id(step)},
            )
            copy.start()
            out.append(copy)
        return out

    def gather_lon(which, copies):
        for copy in copies:
            copy.wait()
        out = []
        for step in range(1, lon_n):
            copy = remote(
                ag1.at[which], ag2.at[which, step - 1],
                a2_s.at[which, step - 1], a2_r.at[which, step - 1], {"lon": lon_id(step)},
            )
            copy.start()
            out.append(copy)
        return out

    def finish(which, copies, out):
        part = chans // lon_n
        for step in range(lon_n):
            if step:
                copies[step - 1].wait()
            for f in range(frame_n):
                if step:
                    piece = ag2[which, step - 1, f]
                else:
                    piece = ag1[which, f]
                wide_out[frame_id(-f)] = piece.astype(F32)
            for f in range(frame_n):
                acc[f * chunk : (f + 1) * chunk, :] = wide_out[f]
            out[lon_id(-step)] = acc[0 : 9 * part, :].reshape(9, part, chans).astype(BF)

    for g in range(2):
        block = gext[1 + g * half : 1 + (g + 1) * half, 8 : 8 + WIDE, :]
        block = jnp.where(inside, block, 0.0).reshape(half * WIDE, chans)
        gt[:, g * half * WIDE : (g + 1) * half * WIDE] = block.T.astype(BF)
    second1 = weight_terms(0, xh)

    for g in range(2):
        back = conv(xg, wb, g * half).reshape(half, WIDE, chans)
        active = hext[1 + g * half : 1 + (g + 1) * half, 8 : 8 + WIDE, :] > 0
        block = jnp.where(active & inside, back, 0.0).reshape(half * WIDE, chans)
        gt[:, g * half * WIDE : (g + 1) * half * WIDE] = block.T.astype(BF)
    first1 = weight_terms(1, xx)
    second2 = over_frames(0, second1)

    for step in range(1, lon_n):
        returns[step - 1].wait()
        retall[:, step * cap : (step + 1) * cap] = ret_recv[step - 1]
    home = dot(retall[...], pt[...]).T
    share = tracks // frame_n
    for f in range(frame_n):
        piece = home[f * share : (f + 1) * share, :]
        qg_own[f] = piece
        qg_send[f] = piece.astype(BF)
    qgs = []
    for step in range(1, frame_n):
        copy = remote(
            qg_send.at[frame_id(step)], qg_recv.at[step - 1], qg_s.at[step - 1],
            qg_r.at[step - 1], {"frame": frame_id(step)},
        )
        copy.start()
        qgs.append(copy)

    first2 = over_frames(1, first1)
    second3 = gather_frames(0, second2)
    first3 = gather_frames(1, first2)
    second4 = gather_lon(0, second3)
    total = qg_own[frame]
    for step in range(1, frame_n):
        qgs[step - 1].wait()
        total = total + qg_recv[step - 1].astype(F32)
    query_out[...] = total
    first4 = gather_lon(1, first3)
    finish(0, second4, second_out)
    finish(1, first4, first_out)


def per_device(
    layer_input, hidden_saved, conv_weight, queries, corr_cotangent,
    window_rows, window_cols, owner_strip,
):
    lon_n, frame_n = lax.axis_size("lon"), lax.axis_size("frame")
    _, rows_n, cols_n, chans = hidden_saved.shape
    tracks = queries.shape[0]
    cap = tracks // 4
    slots = lon_n * cap
    part = chans // lon_n
    chunk = -(-9 * part // frame_n)
    scale = 1.0 / math.sqrt(rows_n * cols_n * lon_n * frame_n)
    dims = (lon_n, frame_n, rows_n, cols_n, chans, tracks, cap, chunk, scale)
    share = tracks // frame_n
    vm = pltpu.VMEM
    dma = pltpu.SemaphoreType.DMA
    scratch = [
        vm((rows_n + 2, EXT, chans), F32),
        vm((rows_n + 2, EXT, chans), F32),
        vm((rows_n + 2, EXT, chans), F32),
        vm((rows_n + 2, WIDE, 3 * chans), BF),
        vm((rows_n + 2, WIDE, 3 * chans), BF),
        vm((rows_n + 2, WIDE, 3 * chans), BF),
        vm((rows_n * WIDE, chans), BF),
        vm((3, 3 * chans, chans), BF),
        vm((rows_n, WIDE, chans), F32),
        vm((chans, rows_n * WIDE), BF),
        vm((rows_n * WIDE, slots), BF),
        vm((64, tracks), F32),
        vm((slots, tracks), BF),
        vm((slots, chans), BF),
        vm((64, slots), F32),
        vm((lon_n - 1, cap + 64, chans), BF),
        vm((lon_n - 1, cap + 64, chans), BF),
        vm((2, rows_n, 8, chans), BF),
        vm((2, rows_n, 8, chans), BF),
        vm((2, rows_n, 8, chans), F32),
        vm((2, rows_n, 8, chans), F32),
        vm((lon_n - 1, chans, cap), BF),
        vm((lon_n - 1, chans, cap), BF),
        vm((chans, slots), BF),
        vm((frame_n, share, chans), BF),
        vm((frame_n, share, chans), F32),
        vm((frame_n - 1, share, chans), BF),
        vm((2, 9, chans, chans), F32),
        vm((2, lon_n, 9, part, chans), BF),
        vm((2, lon_n - 1, 9, part, chans), BF),
        vm((chunk * frame_n, chans), F32),
        vm((2, frame_n, chunk, chans), F32),
        vm((2, frame_n, chunk, chans), BF),
        vm((2, frame_n - 1, chunk, chans), BF),
        vm((2, frame_n, chunk, chans), BF),
        vm((2, lon_n - 1, frame_n, chunk, chans), BF),
        vm((frame_n, chunk, chans), F32),
        dma((lon_n - 1,)), dma((lon_n - 1,)),
        dma((2,)), dma((2,)),
        dma((2,)), dma((2,)),
        dma((lon_n - 1,)), dma((lon_n - 1,)),
        dma((frame_n - 1,)), dma((frame_n - 1,)),
        dma((2, lon_n - 1)), dma((2, lon_n - 1)),
        dma((2, frame_n - 1)), dma((2, frame_n - 1)),
        dma((2, frame_n - 1)), dma((2, frame_n - 1)),
        dma((2, lon_n - 1)), dma((2, lon_n - 1)),
    ]
    spec = pl.BlockSpec(memory_space=pltpu.VMEM)
    query_grad, first, second = pl.pallas_call(
        functools.partial(kernel, dims),
        out_shape=(
            jax.ShapeDtypeStruct((share, chans), F32),
            jax.ShapeDtypeStruct((lon_n, 9, part, chans), BF),
            jax.ShapeDtypeStruct((lon_n, 9, part, chans), BF),
        ),
        in_specs=[spec] * 8,
        out_specs=(spec,) * 3,
        scratch_shapes=scratch,
        compiler_params=pltpu.CompilerParams(
            collective_id=0, has_side_effects=True, vmem_limit_bytes=60 * 1024 * 1024
        ),
    )(
        layer_input[0], hidden_saved[0], conv_weight.reshape(3, 3 * chans, chans), queries,
        corr_cotangent[0], window_rows, window_cols, owner_strip[:, :, 0],
    )

    def unfold(value):
        return value.transpose(1, 0, 2, 3).reshape(3, 3, chans, chans).astype(F32)

    return query_grad, unfold(first), unfold(second)


def solution(mesh):
    placed = (
        P("frame", None, "lon", None),
        P("frame", None, "lon", None),
        P(),
        P("lon", None),
        P("frame", None, "lon"),
        P("frame", "lon"),
        P("frame", "lon"),
        P("frame", "lon", None),
    )
    return jax.shard_map(
        per_device,
        mesh=mesh,
        in_specs=placed,
        out_specs=(P(("lon", "frame"), None), P(), P()),
        check_vma=False,
    )
```

```python
import functools
import math

import jax
import jax.numpy as jnp
from jax import lax
from jax.experimental import pallas as pl
from jax.experimental.pallas import tpu as pltpu
from jax.sharding import PartitionSpec as P

WIN = 7
WIDE = 144
EXT = 160
BF = jnp.bfloat16
F32 = jnp.float32
MESH = pl.DeviceIdType.MESH


def dot(a, b):
    return jnp.dot(a, b, preferred_element_type=F32)


def kernel(
    dims,
    x_any, h_any, w_any, q_any, cot_ref, rows_ref, cols_ref, own_ref,
    query_out, first_out, second_out,
    x_ref, h_ref, w_ref, q_ref, hext, xext, gext, xh, xx, xg, feat, wb, fgrad, gt, spread,
    cm, pt, qall, cmall,
    pay_send, pay_recv, halo_send, halo_recv, edge_send, edge_recv,
    ret_send, ret_recv, retall, qg_send, qg_own, qg_recv,
    grads, w1_send, w1_recv, acc, w2_own, w2_send, w2_recv, ag1, ag2, wide_out,
    pay_s, pay_r, halo_s, halo_r, edge_s, edge_r, ret_s, ret_r, qg_s, qg_r,
    w1_s, w1_r, w2_s, w2_r, a1_s, a1_r, a2_s, a2_r, load_s,
):
    lon_n, frame_n, rows_n, cols_n, chans, tracks, cap, chunk, scale = dims
    lon, frame = lax.axis_index("lon"), lax.axis_index("frame")
    half = rows_n // 2
    order = sorted(range(frame_n), key=lambda f: min(f, frame_n - f))

    def lon_id(steps):
        return lax.rem(lon + steps + lon_n, lon_n)

    def frame_id(steps):
        return lax.rem(frame + steps + frame_n, frame_n)

    def remote(src, dst, send, recv, where):
        return pltpu.make_async_remote_copy(
            src_ref=src, dst_ref=dst, send_sem=send, recv_sem=recv,
            device_id=where, device_id_type=MESH,
        )

    barrier = pltpu.get_barrier_semaphore()
    for step in range(1, lon_n):
        pl.semaphore_signal(barrier, inc=1, device_id={"lon": lon_id(step)}, device_id_type=MESH)
    for step in range(1, frame_n):
        pl.semaphore_signal(barrier, inc=1, device_id={"frame": frame_id(step)}, device_id_type=MESH)

    loads = [
        pltpu.make_async_copy(source, target, load_s.at[i])
        for i, (source, target) in enumerate(
            ((q_any, q_ref), (h_any, h_ref), (x_any, x_ref), (w_any, w_ref))
        )
    ]
    for copy in loads:
        copy.start()

    owners = own_ref[...]
    marks = (owners == lax.broadcasted_iota(jnp.int32, (16, tracks), 0)).astype(F32)
    earlier = (
        lax.broadcasted_iota(jnp.int32, (tracks, tracks), 0)
        < lax.broadcasted_iota(jnp.int32, (tracks, tracks), 1)
    ).astype(F32).astype(BF)
    before = dot(marks.astype(BF), earlier)
    rank = jnp.sum(before * marks, axis=0, keepdims=True).astype(jnp.int32)
    slot = owners * cap + rank
    cm[...] = jnp.zeros_like(cm)
    for i in range(WIN):
        cm[8 * i : 8 * i + WIN, :] = cot_ref[WIN * i : WIN * i + WIN, :].astype(F32)
    cm[56:57, :] = rows_ref[...].astype(F32)
    cm[57:58, :] = (cols_ref[...] + 3).astype(F32)
    cm_half = cm[...].astype(BF)

    loads[0].wait()
    for step in range(lon_n):
        local = slot - lon_id(step) * cap
        hot = (local == lax.broadcasted_iota(jnp.int32, (cap, tracks), 0)).astype(F32).astype(BF)
        pt[step * cap : (step + 1) * cap, :] = hot
        q_part = dot(hot, q_ref[...]).astype(BF)
        c_part = lax.dot_general(
            cm_half, hot, (((1,), (1,)), ((), ())), preferred_element_type=F32
        )
        if step:
            pay_send[step - 1, 0:cap, :] = q_part
            pay_send[step - 1, cap : cap + 64, :] = c_part.astype(BF)
        else:
            qall[0:cap, :] = q_part
            cmall[:, 0:cap] = c_part

    loads[1].wait()
    loads[2].wait()
    halo_send[...] = jnp.zeros_like(halo_send)
    halo_send[0, :, 0:4] = h_ref[:, cols_n - 8 :].astype(F32)[:, 4:8].astype(BF)
    halo_send[0, :, 4:5] = x_ref[:, cols_n - 8 :].astype(F32)[:, 7:8].astype(BF)
    halo_send[1, :, 0:4] = h_ref[:, 0:8].astype(F32)[:, 0:4].astype(BF)
    halo_send[1, :, 4:5] = x_ref[:, 0:8].astype(F32)[:, 0:1].astype(BF)

    loads[3].wait()
    for a in range(3):
        for b in range(3):
            tap = w_ref[2 - a, (2 - b) * chans : (3 - b) * chans, :].astype(F32)
            wb[a, b * chans : (b + 1) * chans, :] = tap.T.astype(BF)

    def spread_block(step):
        lanes = slice(step * cap, (step + 1) * cap)
        rows_t = cmall[56:57, lanes].astype(jnp.int32)
        cols_t = cmall[57:58, lanes].astype(jnp.int32) + 5
        placed = []
        for r in range(rows_n):
            value = jnp.zeros((8, cap), F32)
            for i in range(WIN):
                if 0 <= r - i <= rows_n - WIN:
                    value = jnp.where(rows_t == r - i, cmall[8 * i : 8 * i + 8, lanes], value)
            placed.append(value)

        @pl.loop(0, WIDE // 16)
        def _(tile):
            offset = lax.broadcasted_iota(jnp.int32, (16, cap), 0) + tile * 16 - cols_t
            hits = [offset == j for j in range(WIN)]
            for r in range(rows_n):
                value = jnp.zeros((16, cap), F32)
                for j in range(WIN):
                    value = jnp.where(hits[j], placed[r][j : j + 1, :], value)
                start = pl.multiple_of(r * WIDE + tile * 16, 16)
                spread[pl.ds(start, 16), lanes] = value.astype(BF)

    def fill(ext, src):
        ext[...] = jnp.zeros_like(ext)

        @pl.loop(0, rows_n)
        def _(r):
            ext[r + 1, 16 : 16 + cols_n, :] = src[r].astype(F32)

    def side_by_side(ext, out):
        @pl.loop(0, rows_n + 2)
        def _(r):
            for b in range(3):
                out[r, :, b * chans : (b + 1) * chans] = ext[r, 7 + b : 7 + b + WIDE, :].astype(BF)

    fill(hext, h_ref)
    fill(xext, x_ref)

    pl.semaphore_wait(barrier, lon_n - 1 + frame_n - 1)
    halos = [
        remote(halo_send.at[0], halo_recv.at[0], halo_s.at[0], halo_r.at[0], {"lon": lon_id(1)}),
        remote(halo_send.at[1], halo_recv.at[1], halo_s.at[1], halo_r.at[1], {"lon": lon_id(-1)}),
    ]
    for copy in halos:
        copy.start()
    pays = [
        remote(
            pay_send.at[step - 1], pay_recv.at[step - 1], pay_s.at[step - 1],
            pay_r.at[step - 1], {"lon": lon_id(step)},
        )
        for step in range(1, lon_n)
    ]
    for copy in pays:
        copy.start()
    spread_block(0)
    for copy in halos:
        copy.wait()
    prior = halo_recv[0].astype(F32)
    later = halo_recv[1].astype(F32)
    hext[1 : rows_n + 1, 12:16, :] = prior[:, 0:4]
    hext[1 : rows_n + 1, 16 + cols_n : 20 + cols_n, :] = later[:, 0:4]
    xext[1 : rows_n + 1, 15:16, :] = prior[:, 4:5]
    xext[1 : rows_n + 1, 16 + cols_n : 17 + cols_n, :] = later[:, 4:5]
    side_by_side(hext, xh)

    def conv(source, weight, r0):
        total = None
        for a in range(3):
            block = source[r0 + a : r0 + a + half].reshape(half * WIDE, 3 * chans)
            term = dot(block, weight[a])
            total = term if total is None else total + term
        return total

    for g in range(2):
        feat[g * half * WIDE : (g + 1) * half * WIDE, :] = conv(xh, w_ref, g * half).astype(BF)
    side_by_side(xext, xx)

    for step in range(1, lon_n):
        pays[step - 1].wait()
        qall[step * cap : (step + 1) * cap, :] = pay_recv[step - 1, 0:cap, :]
        cmall[:, step * cap : (step + 1) * cap] = pay_recv[step - 1, cap : cap + 64, :].astype(F32)
        spread_block(step)

    for g in range(2):
        cells = slice(g * half * WIDE, (g + 1) * half * WIDE)
        fgrad[g * half : (g + 1) * half] = dot(spread[cells, :], qall[...]).reshape(
            half, WIDE, chans
        )
    edge_send[0, :, 0:4] = fgrad[:, 7 + cols_n : 11 + cols_n, :]
    edge_send[1, :, 0:4] = fgrad[:, 5:9, :]
    edge_send[:, :, 4:8] = jnp.zeros((2, rows_n, 4, chans), F32)
    edges = [
        remote(edge_send.at[0], edge_recv.at[0], edge_s.at[0], edge_r.at[0], {"lon": lon_id(1)}),
        remote(edge_send.at[1], edge_recv.at[1], edge_s.at[1], edge_r.at[1], {"lon": lon_id(-1)}),
    ]
    for copy in edges:
        copy.start()

    slot_grads = lax.dot_general(
        feat[...], spread[...], (((0,), (0,)), ((), ())), preferred_element_type=F32
    )
    retall[:, 0:cap] = slot_grads[:, 0:cap].astype(BF)
    returns = []
    for step in range(1, lon_n):
        ret_send[step - 1] = slot_grads[:, step * cap : (step + 1) * cap].astype(BF)
        copy = remote(
            ret_send.at[step - 1], ret_recv.at[step - 1], ret_s.at[step - 1],
            ret_r.at[step - 1], {"lon": lon_id(-step)},
        )
        copy.start()
        returns.append(copy)

    gext[...] = jnp.zeros_like(gext)
    for copy in edges:
        copy.wait()
    gext[1 : rows_n + 1, 16 : 16 + cols_n, :] = fgrad[:, 8 : 8 + cols_n, :]
    gext[1 : rows_n + 1, 15:19, :] = fgrad[:, 7:11, :] + edge_recv[0, :, 0:4]
    gext[1 : rows_n + 1, 13 + cols_n : 17 + cols_n, :] = (
        fgrad[:, 5 + cols_n : 9 + cols_n, :] + edge_recv[1, :, 0:4]
    )
    side_by_side(gext, xg)

    column = lax.broadcasted_iota(jnp.int32, (half, WIDE, chans), 1)
    inside = (column >= 8) & (column < 8 + cols_n)

    def weight_terms(which, source):
        copies = []
        for a in range(3):
            block = source[a : a + rows_n].reshape(rows_n * WIDE, 3 * chans)
            term = dot(gt[...], block) * scale
            for b in range(3):
                tap = term[:, b * chans : (b + 1) * chans].T
                grads[which, 3 * a + b] = tap
                for d in range(lon_n):
                    part = tap[d * (chans // lon_n) : (d + 1) * (chans // lon_n), :]
                    w1_send[which, d, 3 * a + b] = part.astype(BF)
            for step in range(1, lon_n):
                copy = remote(
                    w1_send.at[which, lon_id(step), pl.ds(3 * a, 3)],
                    w1_recv.at[which, step - 1, pl.ds(3 * a, 3)],
                    w1_s.at[which, a, step - 1], w1_r.at[which, a, step - 1],
                    {"lon": lon_id(step)},
                )
                copy.start()
                copies.append(copy)
        return copies

    def over_frames(which, copies):
        part = chans // lon_n
        total = grads[which, :, pl.ds(pl.multiple_of(lon * part, part), part), :]
        for copy in copies:
            copy.wait()
        for step in range(1, lon_n):
            total = total + w1_recv[which, step - 1].astype(F32)
        if chunk * frame_n > 9 * part:
            acc[...] = jnp.zeros_like(acc)
        acc[0 : 9 * part, :] = total.reshape(9 * part, chans)
        for f in range(frame_n):
            piece = acc[f * chunk : (f + 1) * chunk, :]
            w2_own[which, f] = piece
            w2_send[which, f] = piece.astype(BF)
        out = []
        for step in range(1, frame_n):
            copy = remote(
                w2_send.at[which, frame_id(step)], w2_recv.at[which, step - 1],
                w2_s.at[which, step - 1], w2_r.at[which, step - 1], {"frame": frame_id(step)},
            )
            copy.start()
            out.append(copy)
        return out

    def gather_frames(which, copies):
        total = w2_own[which, frame]
        for step in range(1, frame_n):
            copies[step - 1].wait()
            total = total + w2_recv[which, step - 1].astype(F32)
        ag1[which, 0] = total.astype(BF)
        out = []
        for step in range(1, frame_n):
            copy = remote(
                ag1.at[which, 0], ag1.at[which, step],
                a1_s.at[which, step - 1], a1_r.at[which, step - 1], {"frame": frame_id(step)},
            )
            copy.start()
            out.append(copy)
        return out

    def gather_lon(which, copies):
        out = []
        for f in order:
            if f:
                copies[f - 1].wait()
            for step in range(1, lon_n):
                copy = remote(
                    ag1.at[which, f], ag2.at[which, step - 1, f],
                    a2_s.at[which, step - 1, f], a2_r.at[which, step - 1, f],
                    {"lon": lon_id(step)},
                )
                copy.start()
                out.append(copy)
        return out

    def finish(which, copies, out):
        part = chans // lon_n
        for copy in copies:
            copy.wait()
        for step in range(lon_n):
            for f in range(frame_n):
                if step:
                    piece = ag2[which, step - 1, f]
                else:
                    piece = ag1[which, f]
                wide_out[frame_id(-f)] = piece.astype(F32)
            for f in range(frame_n):
                acc[f * chunk : (f + 1) * chunk, :] = wide_out[f]
            start = pl.multiple_of(lon_id(-step) * part, part)
            grads[which, :, pl.ds(start, part), :] = acc[0 : 9 * part, :].reshape(9, part, chans)
        out[...] = grads[which].astype(BF)

    for g in range(2):
        block = gext[1 + g * half : 1 + (g + 1) * half, 8 : 8 + WIDE, :]
        block = jnp.where(inside, block, 0.0).reshape(half * WIDE, chans)
        gt[:, g * half * WIDE : (g + 1) * half * WIDE] = block.T.astype(BF)
    second1 = weight_terms(0, xh)

    for g in range(2):
        back = conv(xg, wb, g * half).reshape(half, WIDE, chans)
        active = hext[1 + g * half : 1 + (g + 1) * half, 8 : 8 + WIDE, :] > 0
        block = jnp.where(active & inside, back, 0.0).reshape(half * WIDE, chans)
        gt[:, g * half * WIDE : (g + 1) * half * WIDE] = block.T.astype(BF)
    first1 = weight_terms(1, xx)
    second2 = over_frames(0, second1)

    for step in range(1, lon_n):
        returns[step - 1].wait()
        retall[:, step * cap : (step + 1) * cap] = ret_recv[step - 1]
    home = dot(retall[...], pt[...]).T
    share = tracks // frame_n
    for f in range(frame_n):
        piece = home[f * share : (f + 1) * share, :]
        qg_own[f] = piece
        qg_send[f] = piece.astype(BF)
    qgs = []
    for step in range(1, frame_n):
        copy = remote(
            qg_send.at[frame_id(step)], qg_recv.at[step - 1], qg_s.at[step - 1],
            qg_r.at[step - 1], {"frame": frame_id(step)},
        )
        copy.start()
        qgs.append(copy)

    first2 = over_frames(1, first1)
    second3 = gather_frames(0, second2)
    first3 = gather_frames(1, first2)
    second4 = gather_lon(0, second3)
    total = qg_own[frame]
    for step in range(1, frame_n):
        qgs[step - 1].wait()
        total = total + qg_recv[step - 1].astype(F32)
    query_out[...] = total
    first4 = gather_lon(1, first3)
    finish(0, second4, second_out)
    finish(1, first4, first_out)


def per_device(
    layer_input, hidden_saved, conv_weight, queries, corr_cotangent,
    window_rows, window_cols, owner_strip,
):
    lon_n, frame_n = lax.axis_size("lon"), lax.axis_size("frame")
    _, rows_n, cols_n, chans = hidden_saved.shape
    tracks = queries.shape[0]
    cap = tracks // 4
    slots = lon_n * cap
    part = chans // lon_n
    chunk = -(-9 * part // frame_n)
    scale = 1.0 / math.sqrt(rows_n * cols_n * lon_n * frame_n)
    dims = (lon_n, frame_n, rows_n, cols_n, chans, tracks, cap, chunk, scale)
    share = tracks // frame_n
    vm = pltpu.VMEM
    dma = pltpu.SemaphoreType.DMA
    scratch = [
        vm((rows_n, cols_n, chans), BF),
        vm((rows_n, cols_n, chans), BF),
        vm((3, 3 * chans, chans), BF),
        vm((tracks, chans), BF),
        vm((rows_n + 2, EXT, chans), F32),
        vm((rows_n + 2, EXT, chans), F32),
        vm((rows_n + 2, EXT, chans), F32),
        vm((rows_n + 2, WIDE, 3 * chans), BF),
        vm((rows_n + 2, WIDE, 3 * chans), BF),
        vm((rows_n + 2, WIDE, 3 * chans), BF),
        vm((rows_n * WIDE, chans), BF),
        vm((3, 3 * chans, chans), BF),
        vm((rows_n, WIDE, chans), F32),
        vm((chans, rows_n * WIDE), BF),
        vm((rows_n * WIDE, slots), BF),
        vm((64, tracks), F32),
        vm((slots, tracks), BF),
        vm((slots, chans), BF),
        vm((64, slots), F32),
        vm((lon_n - 1, cap + 64, chans), BF),
        vm((lon_n - 1, cap + 64, chans), BF),
        vm((2, rows_n, 8, chans), BF),
        vm((2, rows_n, 8, chans), BF),
        vm((2, rows_n, 8, chans), F32),
        vm((2, rows_n, 8, chans), F32),
        vm((lon_n - 1, chans, cap), BF),
        vm((lon_n - 1, chans, cap), BF),
        vm((chans, slots), BF),
        vm((frame_n, share, chans), BF),
        vm((frame_n, share, chans), F32),
        vm((frame_n - 1, share, chans), BF),
        vm((2, 9, chans, chans), F32),
        vm((2, lon_n, 9, part, chans), BF),
        vm((2, lon_n - 1, 9, part, chans), BF),
        vm((chunk * frame_n, chans), F32),
        vm((2, frame_n, chunk, chans), F32),
        vm((2, frame_n, chunk, chans), BF),
        vm((2, frame_n - 1, chunk, chans), BF),
        vm((2, frame_n, chunk, chans), BF),
        vm((2, lon_n - 1, frame_n, chunk, chans), BF),
        vm((frame_n, chunk, chans), F32),
        dma((lon_n - 1,)), dma((lon_n - 1,)),
        dma((2,)), dma((2,)),
        dma((2,)), dma((2,)),
        dma((lon_n - 1,)), dma((lon_n - 1,)),
        dma((frame_n - 1,)), dma((frame_n - 1,)),
        dma((2, 3, lon_n - 1)), dma((2, 3, lon_n - 1)),
        dma((2, frame_n - 1)), dma((2, frame_n - 1)),
        dma((2, frame_n - 1)), dma((2, frame_n - 1)),
        dma((2, lon_n - 1, frame_n)), dma((2, lon_n - 1, frame_n)),
        dma((4,)),
    ]
    spec = pl.BlockSpec(memory_space=pltpu.VMEM)
    query_grad, first, second = pl.pallas_call(
        functools.partial(kernel, dims),
        out_shape=(
            jax.ShapeDtypeStruct((share, chans), F32),
            jax.ShapeDtypeStruct((9, chans, chans), BF),
            jax.ShapeDtypeStruct((9, chans, chans), BF),
        ),
        in_specs=[pl.BlockSpec(memory_space=pl.ANY)] * 4 + [spec] * 4,
        out_specs=(spec,) * 3,
        scratch_shapes=scratch,
        compiler_params=pltpu.CompilerParams(
            collective_id=0, has_side_effects=True, vmem_limit_bytes=60 * 1024 * 1024
        ),
    )(
        layer_input[0], hidden_saved[0], conv_weight.reshape(3, 3 * chans, chans), queries,
        corr_cotangent[0], window_rows, window_cols, owner_strip[:, :, 0],
    )

    def unfold(value):
        return value.reshape(3, 3, chans, chans).astype(F32)

    return query_grad, unfold(first), unfold(second)


def solution(mesh):
    placed = (
        P("frame", None, "lon", None),
        P("frame", None, "lon", None),
        P(),
        P("lon", None),
        P("frame", None, "lon"),
        P("frame", "lon"),
        P("frame", "lon"),
        P("frame", "lon", None),
    )
    return jax.shard_map(
        per_device,
        mesh=mesh,
        in_specs=placed,
        out_specs=(P(("lon", "frame"), None), P(), P()),
        check_vma=False,
    )
```

```python
import functools
import math

import jax
import jax.numpy as jnp
from jax import lax
from jax.experimental import pallas as pl
from jax.experimental.pallas import tpu as pltpu
from jax.sharding import PartitionSpec as P

WIN = 7
WIDE = 144
EXT = 160
BF = jnp.bfloat16
F32 = jnp.float32
MESH = pl.DeviceIdType.MESH


def dot(a, b):
    return jnp.dot(a, b, preferred_element_type=F32)


def kernel(
    dims,
    x_any, h_any, w_any, q_any, cot_ref, rows_ref, cols_ref, own_ref,
    query_out, first_out, second_out,
    x_ref, h_ref, w_ref, q_ref, hext, xext, gext, xh, xx, xg, feat, wb, fgrad, gt, spread,
    cm, pt, qall, cmall,
    pay_send, pay_recv, halo_send, halo_recv, edge_send, edge_recv,
    ret_send, ret_recv, retall, qg_send, qg_own, qg_recv,
    grads, w1_send, w1_recv, acc, w2_own, w2_send, w2_recv, ag1, ag2, wide_out,
    pay_s, pay_r, halo_s, halo_r, edge_s, edge_r, ret_s, ret_r, qg_s, qg_r,
    w1_s, w1_r, w2_s, w2_r, a1_s, a1_r, a2_s, a2_r, load_s,
):
    lon_n, frame_n, rows_n, cols_n, chans, tracks, cap, chunk, scale = dims
    lon, frame = lax.axis_index("lon"), lax.axis_index("frame")
    half = rows_n // 2
    order = sorted(range(frame_n), key=lambda f: min(f, frame_n - f))

    def lon_id(steps):
        return lax.rem(lon + steps + lon_n, lon_n)

    def frame_id(steps):
        return lax.rem(frame + steps + frame_n, frame_n)

    def remote(src, dst, send, recv, where):
        return pltpu.make_async_remote_copy(
            src_ref=src, dst_ref=dst, send_sem=send, recv_sem=recv,
            device_id=where, device_id_type=MESH,
        )

    barrier = pltpu.get_barrier_semaphore()
    for step in range(1, lon_n):
        pl.semaphore_signal(barrier, inc=1, device_id={"lon": lon_id(step)}, device_id_type=MESH)
    for step in range(1, frame_n):
        pl.semaphore_signal(barrier, inc=1, device_id={"frame": frame_id(step)}, device_id_type=MESH)

    loads = [
        pltpu.make_async_copy(source, target, load_s.at[i])
        for i, (source, target) in enumerate(
            ((q_any, q_ref), (h_any, h_ref), (x_any, x_ref), (w_any, w_ref))
        )
    ]
    for copy in loads:
        copy.start()

    owners = own_ref[...]
    marks = (owners == lax.broadcasted_iota(jnp.int32, (16, tracks), 0)).astype(F32)
    earlier = (
        lax.broadcasted_iota(jnp.int32, (tracks, tracks), 0)
        < lax.broadcasted_iota(jnp.int32, (tracks, tracks), 1)
    ).astype(F32).astype(BF)
    before = dot(marks.astype(BF), earlier)
    rank = jnp.sum(before * marks, axis=0, keepdims=True).astype(jnp.int32)
    slot = owners * cap + rank
    cm[...] = jnp.zeros_like(cm)
    for i in range(WIN):
        cm[8 * i : 8 * i + WIN, :] = cot_ref[WIN * i : WIN * i + WIN, :].astype(F32)
    cm[56:57, :] = rows_ref[...].astype(F32)
    cm[57:58, :] = (cols_ref[...] + 3).astype(F32)
    cm_half = cm[...].astype(BF)

    loads[0].wait()
    for step in range(lon_n):
        local = slot - lon_id(step) * cap
        hot = (local == lax.broadcasted_iota(jnp.int32, (cap, tracks), 0)).astype(F32).astype(BF)
        pt[step * cap : (step + 1) * cap, :] = hot
        q_part = dot(hot, q_ref[...]).astype(BF)
        c_part = lax.dot_general(
            cm_half, hot, (((1,), (1,)), ((), ())), preferred_element_type=F32
        )
        if step:
            pay_send[step - 1, 0:cap, :] = q_part
            pay_send[step - 1, cap : cap + 64, :] = c_part.astype(BF)
        else:
            qall[0:cap, :] = q_part
            cmall[:, 0:cap] = c_part

    loads[1].wait()
    loads[2].wait()
    halo_send[...] = jnp.zeros_like(halo_send)
    halo_send[0, :, 0:4] = h_ref[:, cols_n - 8 :].astype(F32)[:, 4:8].astype(BF)
    halo_send[0, :, 4:5] = x_ref[:, cols_n - 8 :].astype(F32)[:, 7:8].astype(BF)
    halo_send[1, :, 0:4] = h_ref[:, 0:8].astype(F32)[:, 0:4].astype(BF)
    halo_send[1, :, 4:5] = x_ref[:, 0:8].astype(F32)[:, 0:1].astype(BF)

    loads[3].wait()
    for a in range(3):
        for b in range(3):
            tap = w_ref[2 - a, (2 - b) * chans : (3 - b) * chans, :].astype(F32)
            wb[a, b * chans : (b + 1) * chans, :] = tap.T.astype(BF)

    def spread_block(step):
        lanes = slice(step * cap, (step + 1) * cap)
        rows_t = cmall[56:57, lanes].astype(jnp.int32)
        cols_t = cmall[57:58, lanes].astype(jnp.int32) + 5
        placed = []
        for r in range(rows_n):
            value = jnp.zeros((8, cap), F32)
            for i in range(WIN):
                if 0 <= r - i <= rows_n - WIN:
                    value = jnp.where(rows_t == r - i, cmall[8 * i : 8 * i + 8, lanes], value)
            placed.append(value)

        @pl.loop(0, WIDE // 16)
        def _(tile):
            offset = lax.broadcasted_iota(jnp.int32, (16, cap), 0) + tile * 16 - cols_t
            hits = [offset == j for j in range(WIN)]
            for r in range(rows_n):
                value = jnp.zeros((16, cap), F32)
                for j in range(WIN):
                    value = jnp.where(hits[j], placed[r][j : j + 1, :], value)
                start = pl.multiple_of(r * WIDE + tile * 16, 16)
                spread[pl.ds(start, 16), lanes] = value.astype(BF)

    def fill(ext, src):
        ext[...] = jnp.zeros_like(ext)

        @pl.loop(0, rows_n)
        def _(r):
            ext[r + 1, 16 : 16 + cols_n, :] = src[r].astype(F32)

    def side_by_side(ext, out):
        @pl.loop(0, rows_n + 2)
        def _(r):
            for b in range(3):
                out[r, :, b * chans : (b + 1) * chans] = ext[r, 7 + b : 7 + b + WIDE, :].astype(BF)

    fill(hext, h_ref)
    fill(xext, x_ref)

    pl.semaphore_wait(barrier, lon_n - 1 + frame_n - 1)
    halos = [
        remote(halo_send.at[0], halo_recv.at[0], halo_s.at[0], halo_r.at[0], {"lon": lon_id(1)}),
        remote(halo_send.at[1], halo_recv.at[1], halo_s.at[1], halo_r.at[1], {"lon": lon_id(-1)}),
    ]
    for copy in halos:
        copy.start()
    pays = [
        remote(
            pay_send.at[step - 1], pay_recv.at[step - 1], pay_s.at[step - 1],
            pay_r.at[step - 1], {"lon": lon_id(step)},
        )
        for step in range(1, lon_n)
    ]
    for copy in pays:
        copy.start()
    spread_block(0)
    for copy in halos:
        copy.wait()
    prior = halo_recv[0].astype(F32)
    later = halo_recv[1].astype(F32)
    hext[1 : rows_n + 1, 12:16, :] = prior[:, 0:4]
    hext[1 : rows_n + 1, 16 + cols_n : 20 + cols_n, :] = later[:, 0:4]
    xext[1 : rows_n + 1, 15:16, :] = prior[:, 4:5]
    xext[1 : rows_n + 1, 16 + cols_n : 17 + cols_n, :] = later[:, 4:5]
    side_by_side(hext, xh)

    def conv(source, weight, r0):
        total = None
        for a in range(3):
            block = source[r0 + a : r0 + a + half].reshape(half * WIDE, 3 * chans)
            term = dot(block, weight[a])
            total = term if total is None else total + term
        return total

    for g in range(2):
        feat[g * half * WIDE : (g + 1) * half * WIDE, :] = conv(xh, w_ref, g * half).astype(BF)
    side_by_side(xext, xx)

    for step in range(1, lon_n):
        pays[step - 1].wait()
        qall[step * cap : (step + 1) * cap, :] = pay_recv[step - 1, 0:cap, :]
        cmall[:, step * cap : (step + 1) * cap] = pay_recv[step - 1, cap : cap + 64, :].astype(F32)
        spread_block(step)

    for g in range(2):
        cells = slice(g * half * WIDE, (g + 1) * half * WIDE)
        fgrad[g * half : (g + 1) * half] = dot(spread[cells, :], qall[...]).reshape(
            half, WIDE, chans
        )
    edge_send[0, :, 0:4] = fgrad[:, 7 + cols_n : 11 + cols_n, :]
    edge_send[1, :, 0:4] = fgrad[:, 5:9, :]
    edge_send[:, :, 4:8] = jnp.zeros((2, rows_n, 4, chans), F32)
    edges = [
        remote(edge_send.at[0], edge_recv.at[0], edge_s.at[0], edge_r.at[0], {"lon": lon_id(1)}),
        remote(edge_send.at[1], edge_recv.at[1], edge_s.at[1], edge_r.at[1], {"lon": lon_id(-1)}),
    ]
    for copy in edges:
        copy.start()

    slot_grads = lax.dot_general(
        feat[...], spread[...], (((0,), (0,)), ((), ())), preferred_element_type=F32
    )
    retall[:, 0:cap] = slot_grads[:, 0:cap].astype(BF)
    returns = []
    for step in range(1, lon_n):
        ret_send[step - 1] = slot_grads[:, step * cap : (step + 1) * cap].astype(BF)
        copy = remote(
            ret_send.at[step - 1], ret_recv.at[step - 1], ret_s.at[step - 1],
            ret_r.at[step - 1], {"lon": lon_id(-step)},
        )
        copy.start()
        returns.append(copy)

    gext[...] = jnp.zeros_like(gext)
    for copy in edges:
        copy.wait()
    gext[1 : rows_n + 1, 16 : 16 + cols_n, :] = fgrad[:, 8 : 8 + cols_n, :]
    gext[1 : rows_n + 1, 15:19, :] = fgrad[:, 7:11, :] + edge_recv[0, :, 0:4]
    gext[1 : rows_n + 1, 13 + cols_n : 17 + cols_n, :] = (
        fgrad[:, 5 + cols_n : 9 + cols_n, :] + edge_recv[1, :, 0:4]
    )
    side_by_side(gext, xg)

    column = lax.broadcasted_iota(jnp.int32, (half, WIDE, chans), 1)
    inside = (column >= 8) & (column < 8 + cols_n)

    def weight_terms(which, source):
        copies = []
        for a in range(3):
            block = source[a : a + rows_n].reshape(rows_n * WIDE, 3 * chans)
            term = dot(gt[...], block) * scale
            for b in range(3):
                tap = term[:, b * chans : (b + 1) * chans].T
                grads[which, 3 * a + b] = tap
                for d in range(lon_n):
                    part = tap[d * (chans // lon_n) : (d + 1) * (chans // lon_n), :]
                    w1_send[which, d, 3 * a + b] = part.astype(BF)
        for step in range(1, lon_n):
            copy = remote(
                w1_send.at[which, lon_id(step)], w1_recv.at[which, step - 1],
                w1_s.at[which, 0, step - 1], w1_r.at[which, 0, step - 1], {"lon": lon_id(step)},
            )
            copy.start()
            copies.append(copy)
        return copies

    def over_frames(which, copies):
        part = chans // lon_n
        total = grads[which, :, pl.ds(pl.multiple_of(lon * part, part), part), :]
        for copy in copies:
            copy.wait()
        for step in range(1, lon_n):
            total = total + w1_recv[which, step - 1].astype(F32)
        if chunk * frame_n > 9 * part:
            acc[...] = jnp.zeros_like(acc)
        acc[0 : 9 * part, :] = total.reshape(9 * part, chans)
        for f in range(frame_n):
            piece = acc[f * chunk : (f + 1) * chunk, :]
            w2_own[which, f] = piece
            w2_send[which, f] = piece.astype(BF)
        out = []
        for step in range(1, frame_n):
            copy = remote(
                w2_send.at[which, frame_id(step)], w2_recv.at[which, step - 1],
                w2_s.at[which, step - 1], w2_r.at[which, step - 1], {"frame": frame_id(step)},
            )
            copy.start()
            out.append(copy)
        return out

    def gather_frames(which, copies):
        total = w2_own[which, frame]
        for step in range(1, frame_n):
            copies[step - 1].wait()
            total = total + w2_recv[which, step - 1].astype(F32)
        ag1[which, 0] = total.astype(BF)
        out = []
        for step in range(1, frame_n):
            copy = remote(
                ag1.at[which, 0], ag1.at[which, step],
                a1_s.at[which, step - 1], a1_r.at[which, step - 1], {"frame": frame_id(step)},
            )
            copy.start()
            out.append(copy)
        return out

    def gather_lon(which, copies):
        for copy in copies:
            copy.wait()
        out = []
        for step in range(1, lon_n):
            copy = remote(
                ag1.at[which], ag2.at[which, step - 1],
                a2_s.at[which, step - 1, 0], a2_r.at[which, step - 1, 0], {"lon": lon_id(step)},
            )
            copy.start()
            out.append(copy)
        return out

    def finish(which, copies, out):
        part = chans // lon_n
        for copy in copies:
            copy.wait()
        for step in range(lon_n):
            for f in range(frame_n):
                if step:
                    piece = ag2[which, step - 1, f]
                else:
                    piece = ag1[which, f]
                wide_out[frame_id(-f)] = piece.astype(F32)
            for f in range(frame_n):
                acc[f * chunk : (f + 1) * chunk, :] = wide_out[f]
            start = pl.multiple_of(lon_id(-step) * part, part)
            out[:, pl.ds(start, part), :] = acc[0 : 9 * part, :].reshape(9, part, chans)

    for g in range(2):
        block = gext[1 + g * half : 1 + (g + 1) * half, 8 : 8 + WIDE, :]
        block = jnp.where(inside, block, 0.0).reshape(half * WIDE, chans)
        gt[:, g * half * WIDE : (g + 1) * half * WIDE] = block.T.astype(BF)
    second1 = weight_terms(0, xh)

    for g in range(2):
        back = conv(xg, wb, g * half).reshape(half, WIDE, chans)
        active = hext[1 + g * half : 1 + (g + 1) * half, 8 : 8 + WIDE, :] > 0
        block = jnp.where(active & inside, back, 0.0).reshape(half * WIDE, chans)
        gt[:, g * half * WIDE : (g + 1) * half * WIDE] = block.T.astype(BF)
    first1 = weight_terms(1, xx)
    second2 = over_frames(0, second1)

    for step in range(1, lon_n):
        returns[step - 1].wait()
        retall[:, step * cap : (step + 1) * cap] = ret_recv[step - 1]
    home = dot(retall[...], pt[...]).T
    share = tracks // frame_n
    for f in range(frame_n):
        piece = home[f * share : (f + 1) * share, :]
        qg_own[f] = piece
        qg_send[f] = piece.astype(BF)
    qgs = []
    for step in range(1, frame_n):
        copy = remote(
            qg_send.at[frame_id(step)], qg_recv.at[step - 1], qg_s.at[step - 1],
            qg_r.at[step - 1], {"frame": frame_id(step)},
        )
        copy.start()
        qgs.append(copy)

    first2 = over_frames(1, first1)
    second3 = gather_frames(0, second2)
    first3 = gather_frames(1, first2)
    second4 = gather_lon(0, second3)
    total = qg_own[frame]
    for step in range(1, frame_n):
        qgs[step - 1].wait()
        total = total + qg_recv[step - 1].astype(F32)
    query_out[...] = total
    first4 = gather_lon(1, first3)
    finish(0, second4, second_out)
    finish(1, first4, first_out)


def per_device(
    layer_input, hidden_saved, conv_weight, queries, corr_cotangent,
    window_rows, window_cols, owner_strip,
):
    lon_n, frame_n = lax.axis_size("lon"), lax.axis_size("frame")
    _, rows_n, cols_n, chans = hidden_saved.shape
    tracks = queries.shape[0]
    cap = tracks // 4
    slots = lon_n * cap
    part = chans // lon_n
    chunk = -(-9 * part // frame_n)
    scale = 1.0 / math.sqrt(rows_n * cols_n * lon_n * frame_n)
    dims = (lon_n, frame_n, rows_n, cols_n, chans, tracks, cap, chunk, scale)
    share = tracks // frame_n
    vm = pltpu.VMEM
    dma = pltpu.SemaphoreType.DMA
    scratch = [
        vm((rows_n, cols_n, chans), BF),
        vm((rows_n, cols_n, chans), BF),
        vm((3, 3 * chans, chans), BF),
        vm((tracks, chans), BF),
        vm((rows_n + 2, EXT, chans), F32),
        vm((rows_n + 2, EXT, chans), F32),
        vm((rows_n + 2, EXT, chans), F32),
        vm((rows_n + 2, WIDE, 3 * chans), BF),
        vm((rows_n + 2, WIDE, 3 * chans), BF),
        vm((rows_n + 2, WIDE, 3 * chans), BF),
        vm((rows_n * WIDE, chans), BF),
        vm((3, 3 * chans, chans), BF),
        vm((rows_n, WIDE, chans), F32),
        vm((chans, rows_n * WIDE), BF),
        vm((rows_n * WIDE, slots), BF),
        vm((64, tracks), F32),
        vm((slots, tracks), BF),
        vm((slots, chans), BF),
        vm((64, slots), F32),
        vm((lon_n - 1, cap + 64, chans), BF),
        vm((lon_n - 1, cap + 64, chans), BF),
        vm((2, rows_n, 8, chans), BF),
        vm((2, rows_n, 8, chans), BF),
        vm((2, rows_n, 8, chans), F32),
        vm((2, rows_n, 8, chans), F32),
        vm((lon_n - 1, chans, cap), BF),
        vm((lon_n - 1, chans, cap), BF),
        vm((chans, slots), BF),
        vm((frame_n, share, chans), BF),
        vm((frame_n, share, chans), F32),
        vm((frame_n - 1, share, chans), BF),
        vm((2, 9, chans, chans), F32),
        vm((2, lon_n, 9, part, chans), BF),
        vm((2, lon_n - 1, 9, part, chans), BF),
        vm((chunk * frame_n, chans), F32),
        vm((2, frame_n, chunk, chans), F32),
        vm((2, frame_n, chunk, chans), BF),
        vm((2, frame_n - 1, chunk, chans), BF),
        vm((2, frame_n, chunk, chans), BF),
        vm((2, lon_n - 1, frame_n, chunk, chans), BF),
        vm((frame_n, chunk, chans), F32),
        dma((lon_n - 1,)), dma((lon_n - 1,)),
        dma((2,)), dma((2,)),
        dma((2,)), dma((2,)),
        dma((lon_n - 1,)), dma((lon_n - 1,)),
        dma((frame_n - 1,)), dma((frame_n - 1,)),
        dma((2, 3, lon_n - 1)), dma((2, 3, lon_n - 1)),
        dma((2, frame_n - 1)), dma((2, frame_n - 1)),
        dma((2, frame_n - 1)), dma((2, frame_n - 1)),
        dma((2, lon_n - 1, frame_n)), dma((2, lon_n - 1, frame_n)),
        dma((4,)),
    ]
    spec = pl.BlockSpec(memory_space=pltpu.VMEM)
    query_grad, first, second = pl.pallas_call(
        functools.partial(kernel, dims),
        out_shape=(
            jax.ShapeDtypeStruct((share, chans), F32),
            jax.ShapeDtypeStruct((9, chans, chans), F32),
            jax.ShapeDtypeStruct((9, chans, chans), F32),
        ),
        in_specs=[pl.BlockSpec(memory_space=pl.ANY)] * 4 + [spec] * 4,
        out_specs=(spec,) * 3,
        scratch_shapes=scratch,
        compiler_params=pltpu.CompilerParams(
            collective_id=0, has_side_effects=True, vmem_limit_bytes=60 * 1024 * 1024
        ),
    )(
        layer_input[0], hidden_saved[0], conv_weight.reshape(3, 3 * chans, chans), queries,
        corr_cotangent[0], window_rows, window_cols, owner_strip[:, :, 0],
    )

    def unfold(value):
        return value.reshape(3, 3, chans, chans)

    return query_grad, unfold(first), unfold(second)


def solution(mesh):
    placed = (
        P("frame", None, "lon", None),
        P("frame", None, "lon", None),
        P(),
        P("lon", None),
        P("frame", None, "lon"),
        P("frame", "lon"),
        P("frame", "lon"),
        P("frame", "lon", None),
    )
    return jax.shard_map(
        per_device,
        mesh=mesh,
        in_specs=placed,
        out_specs=(P(("lon", "frame"), None), P(), P()),
        check_vma=False,
    )
```
